32 devices in a mesh: ctx: 16 (over z, x, core), chan: 2 (over y).
Axes of the slice: x: 2, y: 2, z: 4, core: 2. Of those that a mesh axis runs over, the one named last changes fastest.
Arguments:
- gated_input: bfloat16 [4096, 8192], P('ctx', 'chan'), may hold values from -6 to 6
- query: bfloat16 [4096, 8192], P('ctx', 'chan'), may hold values from -6 to 6
- out_grad: bfloat16 [4096, 8192], P('ctx', 'chan'), may hold values from -6 to 6
- out_weight: bfloat16 [8192, 8192], P('chan', 'ctx'), may hold values from -0.0625 to 0.0625
- decay_rate: float32 [16, 8192], P(None, 'chan'), may hold values from 2.4414063e-05 to 0.083333333
- residue: float32 [16, 8192], P(None, 'chan'), may hold values from -0.5 to 0.5
Outputs:
- grad_query: bfloat16 [4096, 8192], P('ctx', 'chan')
- grad_input: bfloat16 [4096, 8192], P('ctx', 'chan')
The draws below stay inside these ranges and needn't reach their ends.
All inputs are finite; a program needn't handle non-finite values.
Results may differ from the reference program's by a relative error of at most 0.0013.
Values may be sent and summed in bfloat16 or wider, within the bound.
A program may use at most 576 MiB of HBM per device.

```python
import math
import jax
import jax.numpy as jnp

D = 8192
MODES = 16
SEQ = 4096


def draw_filter(key):
    base_key = jax.random.fold_in(key, 7)
    kind_key, slow_key, middle_key, fast_key, sign_key = jax.random.split(base_key, 5)
    grid_shape = (MODES, D)
    mode_kinds = jax.random.randint(kind_key, grid_shape, 0, 8)

    def spread(sub_key, lower, upper):
        return jnp.exp(jax.random.uniform(sub_key, grid_shape, jnp.float32, math.log(lower), math.log(upper)))
    slow_rate = spread(slow_key, 0.1 / SEQ, 1.5 / SEQ)
    middle_rate = spread(middle_key, 1.5 / SEQ, 1.0 / 64)
    fast_rate = spread(fast_key, 1.0 / 40, 1.0 / 12)
    decay = jnp.where(mode_kinds < 4, slow_rate, jnp.where(mode_kinds < 6, middle_rate, fast_rate))
    amplitude = jax.random.truncated_normal(sign_key, -4.0, 4.0, grid_shape, jnp.float32)
    weights = amplitude * jnp.sqrt(2.0 * decay / MODES)
    return (decay, weights)


def draw_decay_rate(key, part):
    return draw_filter(key)[0]


def draw_residue(key, part):
    return draw_filter(key)[1]


def block_scale(rng, dims, shards, low, largest):
    factor_of, own = 1.0, jax.random.fold_in(rng, 6)
    for position, blocks in shards:
        steps = jnp.exp(jax.random.uniform(jax.random.fold_in(own, position), (blocks,), jnp.float32, low / len(shards), largest / len(shards)))
        factor_of = factor_of * jnp.repeat(steps, dims[position] // blocks).reshape([-1 if axis == position else 1 for axis in range(len(dims))])
    return factor_of


def normal_values(stream_key, dims, scale, reach, cuts=(), kind=jnp.bfloat16):
    values = jax.random.normal(stream_key, dims, jnp.float32) * scale
    if len(cuts) > 0:
        values = block_scale(stream_key, dims, cuts, -0.22, 0.18) * values
    return jnp.clip(values, min=-reach, max=reach).astype(kind)


def setup_inputs(seed: int = 0) -> dict:
    key_of = jax.random.split(jax.random.key(seed), 7)
    gated_input = normal_values(key_of[0], (SEQ, D), 1.0, 6.0, ((0, 16), (1, 2)))
    query = normal_values(key_of[1], (SEQ, D), 1.0, 6.0, ((0, 16), (1, 2)))
    out_grad = normal_values(key_of[2], (SEQ, D), 1.0, 6.0, ((0, 16), (1, 2)))
    out_weight = normal_values(key_of[3], (D, D), D ** -0.5, 0.0625, ((0, 2), (1, 16)))
    decay_rate = draw_decay_rate(jax.random.fold_in(key_of[6], 71), 0)
    residue = draw_residue(jax.random.fold_in(key_of[6], 71), 0)
    return {"gated_input": gated_input, "query": query, "out_grad": out_grad, "out_weight": out_weight, "decay_rate": decay_rate, "residue": residue}


def causal_conv(signal, kernel):
    length = signal.shape[0]
    total = signal.shape[1]
    span = min(total, 1024)
    pieces = []
    for first in range(0, total, span):
        sig_block = signal[:, first:first + span]
        ker_block = kernel[:, first:first + span]
        spectrum = jnp.fft.rfft(sig_block, 2 * length, axis=0) * jnp.fft.rfft(ker_block, 2 * length, axis=0)
        pieces.append(jnp.fft.irfft(spectrum, 2 * length, axis=0)[:length])
    return jnp.concatenate(pieces, axis=1)


def reference(gated_input, query, out_grad, out_weight, decay_rate, residue):
    lag_steps = jnp.arange(SEQ, dtype=jnp.float32)[:, None]
    filter_taps = jnp.zeros((SEQ, D), jnp.float32)
    for mode_index in range(MODES):
        filter_taps = filter_taps + residue[mode_index][None, :] * jnp.exp(-decay_rate[mode_index][None, :] * lag_steps)
    conv_out = causal_conv(gated_input.astype(jnp.float32), filter_taps)
    grad_mixed = jnp.dot(out_grad, out_weight.T, preferred_element_type=jnp.float32)
    grad_query = (grad_mixed * conv_out).astype(jnp.bfloat16)
    grad_conv = grad_mixed * query.astype(jnp.float32)
    grad_input = causal_conv(grad_conv[::-1], filter_taps)[::-1]
    return grad_query, grad_input.astype(jnp.bfloat16)
```

```python
import functools
import jax
import jax.numpy as jnp
from jax import lax
from jax.experimental import pallas as pl
from jax.experimental.pallas import tpu as pltpu
from jax.sharding import PartitionSpec as P

MESH = pl.DeviceIdType.MESH


def decay_rows(dec, scale):
    return jnp.exp(dec * (-scale))


def segment_run(src, dec, res, init, out, length, backward):
    modes = dec.shape[0]
    rate = jnp.exp(-dec)
    rates = [jnp.broadcast_to(rate[m:m + 1], (8, 128)) for m in range(modes)]
    if out is not None:
        gains = [jnp.broadcast_to(res[m:m + 1], (8, 128)) for m in range(modes)]
    unroll = 4

    def body(t, states):
        states = list(states)
        for u in range(unroll):
            tau = t * unroll + u
            if backward:
                tau = length - 1 - tau
            x = src[pl.ds(tau, 8, stride=length), :]
            states = [rates[m] * states[m] + x for m in range(modes)]
            if out is not None:
                terms = [gains[m] * states[m] for m in range(modes)]
                while len(terms) > 1:
                    terms = [terms[q] + terms[q + 1] for q in range(0, len(terms), 2)]
                out[pl.ds(tau, 8, stride=length), :] = terms[0]
        return tuple(states)

    return lax.fori_loop(0, length // unroll, body, tuple(init))


def segment_combine(ends, dec, length, backward):
    row = lax.broadcasted_iota(jnp.int32, (8, 128), 0)
    powers = [decay_rows(dec, float(length * sh)) for sh in (1, 2, 4)]
    enter, total = [], []
    for m, state in enumerate(ends):
        for sh, power in zip((1, 2, 4), powers):
            if backward:
                moved = jnp.where(row < 8 - sh, pltpu.roll(state, 8 - sh, 0), 0.0)
            else:
                moved = jnp.where(row >= sh, pltpu.roll(state, sh, 0), 0.0)
            state = state + power[m:m + 1] * moved
        if backward:
            enter.append(jnp.where(row < 7, pltpu.roll(state, 7, 0), 0.0))
            total.append(state[0:1])
        else:
            enter.append(jnp.where(row >= 1, pltpu.roll(state, 1, 0), 0.0))
            total.append(state[7:8])
    return enter, total


def kernel(cfg, g_ref, w_ref, x_ref, q_ref, dec_ref, res_ref, gq_ref, gi_ref,
           wbuf, gbuf, pbuf, gsend, acc, own, conv, xin, qin, xs, gs, ys, enf, enb, est, pt, oq, oi,
           l_s, g_s, g_r, z_s, z_r, x_s, x_r, s_s, s_r, m_s, m_r, e_s, e_r, t_s, t_r, xi_s, qi_s, oq_s, oi_s):
    C, NK, ck, T, gcols, NG, fb, GP, lag, win, pre, NS, Z = cfg
    L = T // 8
    LG = ck // 128
    modes = dec_ref.shape[0]
    z = lax.axis_index("ctx") // 4
    i = lax.axis_index("ctx")
    j = lax.axis_index("chan")
    zhi = i // 8
    zlo = lax.rem(i // 4, 2)
    xc = lax.rem(i, 4)
    ix = jnp.bitwise_xor(i, 2)
    isib = jnp.bitwise_xor(i, 1)
    iz = jnp.bitwise_xor(i, 8)
    ip = jnp.bitwise_xor(i, 4)

    def remote(src, dst, ss, rs, dev):
        return pltpu.make_async_remote_copy(src_ref=src, dst_ref=dst, send_sem=ss, recv_sem=rs, device_id=dev, device_id_type=MESH)

    barrier = pltpu.get_barrier_semaphore()
    peers = [(jnp.bitwise_xor(i, q), j) for q in (1, 2, 3)]
    peers += [(jnp.bitwise_xor(z, q) * 4 + xc, j) for q in range(1, Z)]
    peers += [(i, lax.rem(j + d, C)) for d in range(1, C)]
    for dev in peers:
        pl.semaphore_signal(barrier, inc=1, device_id=dev, device_id_type=MESH)
    pl.semaphore_wait(barrier, len(peers))

    rp = T // GP
    split = NG == C

    def slot_of(jj):
        return jj if split else (jj // (2 * (NG // 2))) * (NG // 2) + lax.rem(jj, NG // 2)

    def active(jj, half):
        return None if split else lax.rem(jj // (NG // 2), 2) == half

    def guarded(cond, f):
        if cond is None:
            f()
        else:
            pl.when(cond)(f)

    def cols(half):
        return pl.ds(pl.multiple_of(half * gcols, gcols), gcols) if split else pl.ds(0, gcols)

    def rows(p):
        return pl.ds(p * rp, rp)

    def peer(d):
        return (i, lax.rem(j + d, C))

    me_slot = slot_of(j)

    def g_own(p, d):
        return remote(g_ref.at[rows(p), cols(zlo)], gbuf.at[0, me_slot, rows(p), :], g_s.at[0, d, p], g_r.at[0, d, p], peer(d))

    def g_part(p):
        return remote(g_ref.at[rows(p), cols(1 - zlo)], gbuf.at[1, me_slot, rows(p), :], g_s.at[1, 0, p], g_r.at[1, 0, p], (ip, j))

    def g_fwd(p, d):
        return remote(gbuf.at[1, me_slot, rows(p), :], gbuf.at[1, me_slot, rows(p), :], g_s.at[1, d, p], g_r.at[1, d, p], peer(d))

    def g_local():
        return pltpu.make_async_copy(g_ref.at[:, cols(zlo)], gbuf.at[0, me_slot], l_s.at[0])

    def wrows(k):
        return w_ref.at[pl.ds(pl.multiple_of(k * ck, ck), ck), :]

    def wlocal(k):
        return pltpu.make_async_copy(wrows(k), wbuf.at[k, xc, zhi], l_s.at[k + 1])

    def zsend(k):
        return remote(wrows(k), wbuf.at[k, xc, zhi], z_s.at[k], z_r.at[k], (iz, j))

    def zrecv(k):
        return remote(wrows(k), wbuf.at[k, xc, 1 - zhi], z_s.at[k], z_r.at[k], (iz, j))

    def xfwd(k, b):
        zz = zhi if b == 0 else 1 - zhi
        return remote(wbuf.at[k, xc, zz], wbuf.at[k, xc, zz], x_s.at[k, b], x_r.at[k, b], (ix, j))

    def xrecv(k, b):
        zz = zhi if b == 0 else 1 - zhi
        s = jnp.bitwise_xor(xc, 2)
        return remote(wbuf.at[k, s, zz], wbuf.at[k, s, zz], x_s.at[k, b], x_r.at[k, b], (ix, j))

    def sib(k, b):
        s = jnp.bitwise_xor(xc, 2 * b)
        return remote(wbuf.at[k, s], wbuf.at[k, s], s_s.at[k, b], s_r.at[k, b], (isib, j))

    def sibrecv(k, b):
        s = jnp.bitwise_xor(xc, 2 * b + 1)
        return remote(wbuf.at[k, s], wbuf.at[k, s], s_s.at[k, b], s_r.at[k, b], (isib, j))

    def psend(k):
        return remote(gsend.at[lax.rem(k, NS)], pbuf.at[k], m_s.at[k], m_r.at[k], (ip, j))

    mine = active(j, zlo)
    other = active(j, 1 - zlo)

    def start_g():
        def a():
            g_local().start()
        guarded(mine, a)
        for p in range(GP):
            def b():
                g_part(p).start()

            def c():
                for d in range(1, C):
                    g_own(p, d).start()
            guarded(other, b)
            guarded(mine, c)

    start_g()
    for k in range(NK):
        wlocal(k).start()
    for k in range(min(win, NK)):
        zsend(k).start()
    for k in range(min(pre, NK)):
        wlocal(k).wait()
        xfwd(k, 0).start()

    def fwd_g():
        for p in range(GP):
            g_part(p).wait_recv()
            for d in range(1, C):
                g_fwd(p, d).start()
    guarded(mine, fwd_g)

    def g_wait():
        def a():
            g_local().wait()
        guarded(mine, a)
        for d in range(1, C):
            jj = lax.rem(j + C - d, C)
            sl = slot_of(jj)

            def b():
                for p in range(GP):
                    for h in range(2):
                        r = gbuf.at[h, sl, rows(p), :]
                        remote(r, r, g_s.at[h, d, p], g_r.at[h, d, p], (i, jj)).wait_recv()
            guarded(active(jj, zlo), b)

    per = gcols // fb

    def matmul(k):
        sibrecv(k, 0).wait_recv()
        sibrecv(k, 1).wait_recv()

        for u in range(8):
            a = gbuf[:, u // per, :, (u % per) * fb:(u % per + 1) * fb].reshape(2 * T, fb)
            b = wbuf[k, u % 4, u // 4]
            r = lax.dot_general(a, b, (((1,), (1,)), ((), ())), preferred_element_type=jnp.float32)
            if u == 0:
                acc[...] = r
            else:
                acc[...] += r

        @pl.when(k >= NS)
        def _():
            psend(k - NS).wait_send()
        own[lax.rem(k, own.shape[0])] = acc[0:T, :]
        gsend[lax.rem(k, NS)] = acc[T:2 * T, :]
        psend(k).start()

    def step_a(k):
        @pl.when(k + pre < NK)
        def _():
            wlocal(k + pre).wait()
            xfwd(k + pre, 0).start()
        zrecv(k).wait_recv()
        xfwd(k, 1).start()
        sib(k, 0).start()

        @pl.when(k + win < NK)
        def _():
            zsend(k + win).start()

    def step_b(k):
        for b in range(2):
            xrecv(k, b).wait_recv()
        sib(k, 1).start()

    def lanes(k, g):
        return pl.ds(pl.multiple_of(k * ck + g * 128, 128), 128)

    def chunk(k):
        return pl.ds(pl.multiple_of(k * ck, ck), ck)

    def load_x(k):
        sl = lax.rem(k, xin.shape[0])
        return pltpu.make_async_copy(x_ref.at[:, chunk(k)], xin.at[sl], xi_s.at[sl])

    def load_q(k):
        sl = lax.rem(k, qin.shape[0])
        return pltpu.make_async_copy(q_ref.at[:, chunk(k)], qin.at[sl], qi_s.at[sl])

    def store_q(k):
        sl = lax.rem(k, 2)
        return pltpu.make_async_copy(oq.at[sl], gq_ref.at[:, chunk(k)], oq_s.at[sl])

    def store_i(k):
        sl = lax.rem(k, 2)
        return pltpu.make_async_copy(oi.at[sl], gi_ref.at[:, chunk(k)], oi_s.at[sl])

    def plane_send(w, k, q):
        r = est.at[w, k, xc]
        return remote(r, r, e_s.at[w, k, q], e_r.at[w, k, q], (jnp.bitwise_xor(i, q), j))

    def plane_recv(w, k, q):
        r = est.at[w, k, jnp.bitwise_xor(xc, q)]
        return remote(r, r, e_s.at[w, k, q], e_r.at[w, k, q], (jnp.bitwise_xor(i, q), j))

    def line_send(w, k, q):
        r = pt.at[w, k, z]
        return remote(r, r, t_s.at[w, k, q], t_r.at[w, k, q], (jnp.bitwise_xor(z, q) * 4 + xc, j))

    def line_recv(w, k, q):
        zz = jnp.bitwise_xor(z, q)
        r = pt.at[w, k, zz]
        return remote(r, r, t_s.at[w, k, q], t_r.at[w, k, q], (zz * 4 + xc, j))

    def goes(w, q):
        zz = jnp.bitwise_xor(z, q)
        return zz > z if w == 0 else zz < z

    def comes(w, q):
        zz = jnp.bitwise_xor(z, q)
        return zz < z if w == 0 else zz > z

    def first_pass(w, k, src, ring, slot):
        for g in range(LG):
            dec = dec_ref[:, lanes(k, g)]
            zero = [jnp.zeros((8, 128), jnp.float32)] * modes
            ends = segment_run(src.at[slot, g], dec, None, zero, None, L, w == 1)
            enter, total = segment_combine(ends, dec, L, w == 1)
            for m in range(modes):
                ring[slot, g, m] = enter[m]
                est[w, k, xc, m:m + 1, g * 128:(g + 1) * 128] = total[m]
        for q in (1, 2, 3):
            plane_send(w, k, q).start()

    def plane_walk(w, k):
        one = decay_rows(dec_ref[:, chunk(k)], float(T))
        run = jnp.zeros((modes, ck), jnp.float32)
        before = run
        for c in (range(4) if w == 0 else range(3, -1, -1)):
            before = jnp.where(xc == c, run, before)
            run = one * run + est[w, k, c]
        return before, run

    def middle(w, k):
        for q in (1, 2, 3):
            plane_recv(w, k, q).wait_recv()
        pt[w, k, z] = plane_walk(w, k)[1]
        for q in range(1, Z):
            @pl.when(goes(w, q))
            def _():
                line_send(w, k, q).start()

    def second_pass(w, k, src, ring, slot, out):
        for q in range(1, Z):
            @pl.when(comes(w, q))
            def _():
                line_recv(w, k, q).wait_recv()
        dec_all = dec_ref[:, chunk(k)]
        four = decay_rows(dec_all, float(4 * T))
        run = jnp.zeros((modes, ck), jnp.float32)
        far = run
        for zz in (range(Z) if w == 0 else range(Z - 1, -1, -1)):
            far = jnp.where(z == zz, run, far)
            run = four * run + pt[w, k, zz]
        steps = xc if w == 0 else 3 - xc
        entering = plane_walk(w, k)[0] + jnp.exp(dec_all * (-T * steps.astype(jnp.float32))) * far
        row = lax.broadcasted_iota(jnp.int32, (8, 128), 0)
        seg = (row if w == 0 else 7 - row).astype(jnp.float32) * float(-L)
        for g in range(LG):
            dec = dec_ref[:, lanes(k, g)]
            res = res_ref[:, lanes(k, g)]
            init = []
            for m in range(modes):
                carried = entering[m:m + 1, g * 128:(g + 1) * 128]
                init.append(ring[slot, g, m] + jnp.exp(dec[m:m + 1] * seg) * carried)
            segment_run(src.at[slot, g], dec, res, init, out.at[g], L, w == 1)

    def fwd_first(k):
        load_x(k).wait()

        @pl.when(k + 1 < NK)
        def _():
            load_x(k + 1).start()
        slot = lax.rem(k, xs.shape[0])
        v = xin[lax.rem(k, xin.shape[0])].astype(jnp.float32)
        for g in range(LG):
            xs[slot, g] = v[:, g * 128:(g + 1) * 128]
        first_pass(0, k, xs, enf, slot)

    def fwd_second(k):
        second_pass(0, k, xs, enf, lax.rem(k, xs.shape[0]), conv.at[k])

    def back_first(k):
        psend(k).wait_recv()
        load_q(k).wait()

        @pl.when(k + 1 < NK)
        def _():
            load_q(k + 1).start()
        mixed = own[lax.rem(k, own.shape[0])] + pbuf[k]

        @pl.when(k >= 2)
        def _():
            store_q(k - 2).wait()
        slot = lax.rem(k, gs.shape[0])
        gate = qin[lax.rem(k, qin.shape[0])].astype(jnp.float32)
        for g in range(LG):
            sl = slice(g * 128, (g + 1) * 128)
            oq[lax.rem(k, 2), :, sl] = (mixed[:, sl] * conv[k, g]).astype(jnp.bfloat16)
            gs[slot, g] = mixed[:, sl] * gate[:, sl]
        store_q(k).start()
        first_pass(1, k, gs, enb, slot)

    def back_second(k):
        second_pass(1, k, gs, enb, lax.rem(k, gs.shape[0]), ys)

        @pl.when(k >= 2)
        def _():
            store_i(k - 2).wait()
        for g in range(LG):
            oi[lax.rem(k, 2), :, g * 128:(g + 1) * 128] = ys[g].astype(jnp.bfloat16)
        store_i(k).start()

    load_x(0).start()
    load_q(0).start()
    for zz in range(Z):
        @pl.when(zz > z)
        def _():
            pt[0, :, zz] = jnp.zeros((NK, modes, ck), jnp.float32)

        @pl.when(zz < z)
        def _():
            pt[1, :, zz] = jnp.zeros((NK, modes, ck), jnp.float32)

    def span(k, start, behind, f):
        def upto(t):
            return jnp.maximum(jnp.minimum(jnp.minimum(2 * (t - start + 1), t - behind + 1), NK), 0)

        def body(t, c):
            f(t)
            return c
        lax.fori_loop(upto(k - 1), upto(k), body, 0)

    def guard(k, f):
        @pl.when((k >= 0) & (k < NK))
        def _():
            f(k)

    def loop(k, c):
        guard(k, step_a)

        @pl.when(k == lag)
        def _():
            g_wait()
        span(k, lag, 1, matmul)
        guard(k, fwd_first)
        guard(k, step_b)
        guard(k - 1, lambda t: middle(0, t))
        guard(k - 2, fwd_second)
        span(k, lag + 1, 2, back_first)
        span(k, lag + 2, 3, lambda t: middle(1, t))
        span(k, lag + 3, 4, back_second)
        return c
    lax.fori_loop(0, NK + 4, loop, 0)

    def drain(k, c):
        @pl.when(k >= NK - NS)
        def _():
            psend(k).wait_send()

        @pl.when(k >= NK - 2)
        def _():
            store_q(k).wait()
            store_i(k).wait()
        zsend(k).wait_send()
        xfwd(k, 0).wait_send()
        xfwd(k, 1).wait_send()
        sib(k, 0).wait_send()
        sib(k, 1).wait_send()
        for w in range(2):
            for q in (1, 2, 3):
                plane_send(w, k, q).wait_send()
            for q in range(1, Z):
                @pl.when(goes(w, q))
                def _():
                    line_send(w, k, q).wait_send()
        return c
    lax.fori_loop(0, NK, drain, 0)
    for p in range(GP):
        def b():
            g_part(p).wait_send()

        def c():
            for d in range(1, C):
                g_own(p, d).wait_send()
                g_fwd(p, d).wait_send()
        guarded(other, b)
        guarded(mine, c)


def on_device(gated_input, query, out_grad, out_weight, decay_rate, residue, n, C,
              ck=256, GP=4, lag=5, win=2, pre=6, NS=4):
    T, fw = out_grad.shape
    cw, fb = out_weight.shape
    modes = decay_rate.shape[0]
    NK = cw // ck
    Z = n // 4
    lag = min(lag, NK - 1)
    split = n // C >= 8
    gcols, NG = (fw // 2, C) if split else (fw, C // 2)
    NS = min(NS, NK)
    LG = ck // 128
    cfg = (C, NK, ck, T, gcols, NG, fb, GP, lag, win, pre, NS, Z)
    S = pltpu.SemaphoreType.DMA
    bf, f32 = jnp.bfloat16, jnp.float32
    V = pltpu.VMEM
    any_spec = pl.BlockSpec(memory_space=pl.ANY)
    vmem_spec = pl.BlockSpec(memory_space=pltpu.VMEM)
    return pl.pallas_call(
        functools.partial(kernel, cfg),
        out_shape=(jax.ShapeDtypeStruct((T, cw), bf), jax.ShapeDtypeStruct((T, cw), bf)),
        in_specs=[any_spec] * 4 + [vmem_spec] * 2,
        out_specs=(any_spec, any_spec),
        scratch_shapes=[
            V((NK, 4, 2, ck, fb), bf),
            V((2, NG, T, gcols), bf),
            V((NK, T, ck), f32),
            V((NS, T, ck), f32),
            V((2 * T, ck), f32),
            V((6, T, ck), f32),
            V((NK, LG, T, 128), f32),
            V((2, T, ck), bf), V((2, T, ck), bf),
            V((4, LG, T, 128), f32), V((8, LG, T, 128), f32), V((LG, T, 128), f32),
            V((4, LG, modes, 8, 128), f32), V((8, LG, modes, 8, 128), f32),
            V((2, NK, 4, modes, ck), f32), V((2, NK, Z, modes, ck), f32),
            V((2, T, ck), bf), V((2, T, ck), bf),
            S((NK + 1,)),
            S((2, C, GP)), S((2, C, GP)),
            S((NK,)), S((NK,)),
            S((NK, 2)), S((NK, 2)),
            S((NK, 2)), S((NK, 2)),
            S((NK,)), S((NK,)),
            S((2, NK, 4)), S((2, NK, 4)),
            S((2, NK, Z)), S((2, NK, Z)),
            S((2,)), S((2,)), S((2,)), S((2,)),
        ],
        compiler_params=pltpu.CompilerParams(collective_id=0, has_side_effects=True, vmem_limit_bytes=60 * 1024 * 1024),
    )(out_grad, out_weight, gated_input, query, decay_rate, residue)


def solution(mesh):
    return jax.shard_map(
        functools.partial(on_device, n=mesh.shape["ctx"], C=mesh.shape["chan"]),
        mesh=mesh,
        in_specs=(
            P("ctx", "chan"),
            P("ctx", "chan"),
            P("ctx", "chan"),
            P("chan", "ctx"),
            P(None, "chan"),
            P(None, "chan"),
        ),
        out_specs=(P("ctx", "chan"), P("ctx", "chan")),
        check_vma=False,
    )
```

```python
import functools
import jax
import jax.numpy as jnp
from jax import lax
from jax.experimental import pallas as pl
from jax.experimental.pallas import tpu as pltpu
from jax.sharding import PartitionSpec as P

MESH = pl.DeviceIdType.MESH


def decay_rows(dec, scale):
    return jnp.exp(dec * (-scale))


def segment_run(src, dec, res, init, out, length, backward):
    modes = dec.shape[0]
    rate = jnp.exp(-dec)
    rates = [jnp.broadcast_to(rate[m:m + 1], (8, 128)) for m in range(modes)]
    if out is not None:
        gains = [jnp.broadcast_to(res[m:m + 1], (8, 128)) for m in range(modes)]
    unroll = 4

    def body(t, states):
        states = list(states)
        for u in range(unroll):
            tau = t * unroll + u
            if backward:
                tau = length - 1 - tau
            x = src[pl.ds(tau, 8, stride=length), :]
            states = [rates[m] * states[m] + x for m in range(modes)]
            if out is not None:
                terms = [gains[m] * states[m] for m in range(modes)]
                while len(terms) > 1:
                    terms = [terms[q] + terms[q + 1] for q in range(0, len(terms), 2)]
                out[pl.ds(tau, 8, stride=length), :] = terms[0]
        return tuple(states)

    return lax.fori_loop(0, length // unroll, body, tuple(init))


def segment_combine(ends, dec, length, backward):
    row = lax.broadcasted_iota(jnp.int32, (8, 128), 0)
    powers = [decay_rows(dec, float(length * sh)) for sh in (1, 2, 4)]
    enter, total = [], []
    for m, state in enumerate(ends):
        for sh, power in zip((1, 2, 4), powers):
            if backward:
                moved = jnp.where(row < 8 - sh, pltpu.roll(state, 8 - sh, 0), 0.0)
            else:
                moved = jnp.where(row >= sh, pltpu.roll(state, sh, 0), 0.0)
            state = state + power[m:m + 1] * moved
        if backward:
            enter.append(jnp.where(row < 7, pltpu.roll(state, 7, 0), 0.0))
            total.append(state[0:1])
        else:
            enter.append(jnp.where(row >= 1, pltpu.roll(state, 1, 0), 0.0))
            total.append(state[7:8])
    return enter, total


def kernel(cfg, g_ref, w_ref, x_ref, q_ref, dec_ref, res_ref, gq_ref, gi_ref,
           wbuf, gbuf, pbuf, gsend, acc, own, conv, xin, qin, xs, gs, ys, enf, enb, ends, est, pt, entry, oq, oi,
           l_s, g_s, g_r, z_s, z_r, x_s, x_r, s_s, s_r, m_s, m_r, e_s, e_r, t_s, t_r, o_s, o_r, xi_s, qi_s, oq_s, oi_s):
    C, NK, ck, T, gcols, NG, fb, GP, lag, win, pre, NS, Z = cfg
    L = T // 8
    LG = ck // 128
    modes = dec_ref.shape[0]
    z = lax.axis_index("ctx") // 4
    i = lax.axis_index("ctx")
    j = lax.axis_index("chan")
    zhi = i // 8
    zlo = lax.rem(i // 4, 2)
    xc = lax.rem(i, 4)
    ix = jnp.bitwise_xor(i, 2)
    isib = jnp.bitwise_xor(i, 1)
    iz = jnp.bitwise_xor(i, 8)
    ip = jnp.bitwise_xor(i, 4)

    def remote(src, dst, ss, rs, dev):
        return pltpu.make_async_remote_copy(src_ref=src, dst_ref=dst, send_sem=ss, recv_sem=rs, device_id=dev, device_id_type=MESH)

    barrier = pltpu.get_barrier_semaphore()
    peers = [(jnp.bitwise_xor(i, q), j) for q in (1, 2, 3)]
    peers += [(jnp.bitwise_xor(z, q) * 4 + xc, j) for q in range(1, Z)]
    peers += [(i, lax.rem(j + d, C)) for d in range(1, C)]
    for dev in peers:
        pl.semaphore_signal(barrier, inc=1, device_id=dev, device_id_type=MESH)
    pl.semaphore_wait(barrier, len(peers))

    rp = T // GP
    split = NG == C

    def slot_of(jj):
        return jj if split else (jj // (2 * (NG // 2))) * (NG // 2) + lax.rem(jj, NG // 2)

    def active(jj, half):
        return None if split else lax.rem(jj // (NG // 2), 2) == half

    def guarded(cond, f):
        if cond is None:
            f()
        else:
            pl.when(cond)(f)

    def cols(half):
        return pl.ds(pl.multiple_of(half * gcols, gcols), gcols) if split else pl.ds(0, gcols)

    def rows(p):
        return pl.ds(p * rp, rp)

    def peer(d):
        return (i, lax.rem(j + d, C))

    me_slot = slot_of(j)

    def g_own(p, d):
        return remote(g_ref.at[rows(p), cols(zlo)], gbuf.at[0, me_slot, rows(p), :], g_s.at[0, d, p], g_r.at[0, d, p], peer(d))

    def g_part(p):
        return remote(g_ref.at[rows(p), cols(1 - zlo)], gbuf.at[1, me_slot, rows(p), :], g_s.at[1, 0, p], g_r.at[1, 0, p], (ip, j))

    def g_fwd(p, d):
        return remote(gbuf.at[1, me_slot, rows(p), :], gbuf.at[1, me_slot, rows(p), :], g_s.at[1, d, p], g_r.at[1, d, p], peer(d))

    def g_local():
        return pltpu.make_async_copy(g_ref.at[:, cols(zlo)], gbuf.at[0, me_slot], l_s.at[0])

    def wrows(k):
        return w_ref.at[pl.ds(pl.multiple_of(k * ck, ck), ck), :]

    def wlocal(k):
        return pltpu.make_async_copy(wrows(k), wbuf.at[k, xc, zhi], l_s.at[k + 1])

    def zsend(k):
        return remote(wrows(k), wbuf.at[k, xc, zhi], z_s.at[k], z_r.at[k], (iz, j))

    def zrecv(k):
        return remote(wrows(k), wbuf.at[k, xc, 1 - zhi], z_s.at[k], z_r.at[k], (iz, j))

    def xfwd(k, b):
        zz = zhi if b == 0 else 1 - zhi
        return remote(wbuf.at[k, xc, zz], wbuf.at[k, xc, zz], x_s.at[k, b], x_r.at[k, b], (ix, j))

    def xrecv(k, b):
        zz = zhi if b == 0 else 1 - zhi
        s = jnp.bitwise_xor(xc, 2)
        return remote(wbuf.at[k, s, zz], wbuf.at[k, s, zz], x_s.at[k, b], x_r.at[k, b], (ix, j))

    def sib(k, b):
        s = jnp.bitwise_xor(xc, 2 * b)
        return remote(wbuf.at[k, s], wbuf.at[k, s], s_s.at[k, b], s_r.at[k, b], (isib, j))

    def sibrecv(k, b):
        s = jnp.bitwise_xor(xc, 2 * b + 1)
        return remote(wbuf.at[k, s], wbuf.at[k, s], s_s.at[k, b], s_r.at[k, b], (isib, j))

    def psend(k):
        return remote(gsend.at[lax.rem(k, NS)], pbuf.at[k], m_s.at[k], m_r.at[k], (ip, j))

    mine = active(j, zlo)
    other = active(j, 1 - zlo)

    def start_g():
        def a():
            g_local().start()
        guarded(mine, a)
        for p in range(GP):
            def b():
                g_part(p).start()

            def c():
                for d in range(1, C):
                    g_own(p, d).start()
            guarded(other, b)
            guarded(mine, c)

    start_g()
    for k in range(NK):
        wlocal(k).start()
    for k in range(min(win, NK)):
        zsend(k).start()
    for k in range(min(pre, NK)):
        wlocal(k).wait()
        xfwd(k, 0).start()

    def fwd_g():
        for p in range(GP):
            g_part(p).wait_recv()
            for d in range(1, C):
                g_fwd(p, d).start()
    guarded(mine, fwd_g)

    def g_wait():
        def a():
            g_local().wait()
        guarded(mine, a)
        for d in range(1, C):
            jj = lax.rem(j + C - d, C)
            sl = slot_of(jj)

            def b():
                for p in range(GP):
                    for h in range(2):
                        r = gbuf.at[h, sl, rows(p), :]
                        remote(r, r, g_s.at[h, d, p], g_r.at[h, d, p], (i, jj)).wait_recv()
            guarded(active(jj, zlo), b)

    per = gcols // fb

    def matmul(k):
        sibrecv(k, 0).wait_recv()
        sibrecv(k, 1).wait_recv()

        for u in range(8):
            a = gbuf[:, u // per, :, (u % per) * fb:(u % per + 1) * fb].reshape(2 * T, fb)
            b = wbuf[k, u % 4, u // 4]
            r = lax.dot_general(a, b, (((1,), (1,)), ((), ())), preferred_element_type=jnp.float32)
            if u == 0:
                acc[...] = r
            else:
                acc[...] += r

        @pl.when(k >= NS)
        def _():
            psend(k - NS).wait_send()
        own[lax.rem(k, own.shape[0])] = acc[0:T, :]
        gsend[lax.rem(k, NS)] = acc[T:2 * T, :]
        psend(k).start()

    def step_a(k):
        @pl.when(k + pre < NK)
        def _():
            wlocal(k + pre).wait()
            xfwd(k + pre, 0).start()
        zrecv(k).wait_recv()
        xfwd(k, 1).start()
        sib(k, 0).start()

        @pl.when(k + win < NK)
        def _():
            zsend(k + win).start()

    def step_b(k):
        for b in range(2):
            xrecv(k, b).wait_recv()
        sib(k, 1).start()

    def lanes(k, g):
        return pl.ds(pl.multiple_of(k * ck + g * 128, 128), 128)

    def chunk(k):
        return pl.ds(pl.multiple_of(k * ck, ck), ck)

    def load_x(k):
        sl = lax.rem(k, xin.shape[0])
        return pltpu.make_async_copy(x_ref.at[:, chunk(k)], xin.at[sl], xi_s.at[sl])

    def load_q(k):
        sl = lax.rem(k, qin.shape[0])
        return pltpu.make_async_copy(q_ref.at[:, chunk(k)], qin.at[sl], qi_s.at[sl])

    def store_q(k):
        sl = lax.rem(k, 2)
        return pltpu.make_async_copy(oq.at[sl], gq_ref.at[:, chunk(k)], oq_s.at[sl])

    def store_i(k):
        sl = lax.rem(k, 2)
        return pltpu.make_async_copy(oi.at[sl], gi_ref.at[:, chunk(k)], oi_s.at[sl])

    def owner(k):
        return lax.rem(k, 4)

    def end_send(w, k):
        return remote(ends.at[w, k], est.at[w, k // 4, xc], e_s.at[w, k], e_r.at[w, k, xc], (z * 4 + owner(k), j))

    def end_recv(w, k, q):
        c = jnp.bitwise_xor(xc, q)
        return remote(ends.at[w, k], est.at[w, k // 4, c], e_s.at[w, k], e_r.at[w, k, c], (z * 4 + c, j))

    def line_send(w, k, q):
        r = pt.at[w, k // 4, z]
        return remote(r, r, t_s.at[w, k, q], t_r.at[w, k, q], (jnp.bitwise_xor(z, q) * 4 + xc, j))

    def line_recv(w, k, q):
        zz = jnp.bitwise_xor(z, q)
        r = pt.at[w, k // 4, zz]
        return remote(r, r, t_s.at[w, k, q], t_r.at[w, k, q], (zz * 4 + xc, j))

    def enter_send(w, k, q):
        c = jnp.bitwise_xor(xc, q)
        return remote(est.at[w, k // 4, c], entry.at[w, k], o_s.at[w, k, q], o_r.at[w, k], (z * 4 + c, j))

    def enter_recv(w, k):
        return remote(ends.at[w, k], entry.at[w, k], e_s.at[w, k], o_r.at[w, k], (z * 4 + owner(k), j))

    def goes(w, q):
        zz = jnp.bitwise_xor(z, q)
        return zz > z if w == 0 else zz < z

    def comes(w, q):
        zz = jnp.bitwise_xor(z, q)
        return zz < z if w == 0 else zz > z

    def first_pass(w, k, src, ring, slot):
        for g in range(LG):
            dec = dec_ref[:, lanes(k, g)]
            zero = [jnp.zeros((8, 128), jnp.float32)] * modes
            outs = segment_run(src.at[slot, g], dec, None, zero, None, L, w == 1)
            enter, total = segment_combine(outs, dec, L, w == 1)
            for m in range(modes):
                ring[slot, g, m] = enter[m]
                ends[w, k, m:m + 1, g * 128:(g + 1) * 128] = total[m]

        @pl.when(xc == owner(k))
        def _():
            est[w, k // 4, xc] = ends[w, k]

        @pl.when(xc != owner(k))
        def _():
            end_send(w, k).start()

    def middle(w, k):
        @pl.when(xc == owner(k))
        def _():
            for q in (1, 2, 3):
                end_recv(w, k, q).wait_recv()
            one = decay_rows(dec_ref[:, chunk(k)], float(T))
            run = jnp.zeros((modes, ck), jnp.float32)
            for c in (range(4) if w == 0 else range(3, -1, -1)):
                run = one * run + est[w, k // 4, c]
            pt[w, k // 4, z] = run
            for q in range(1, Z):
                @pl.when(goes(w, q))
                def _():
                    line_send(w, k, q).start()

    def late(w, k):
        @pl.when(xc == owner(k))
        def _():
            for q in range(1, Z):
                @pl.when(comes(w, q))
                def _():
                    line_recv(w, k, q).wait_recv()
            dec_all = dec_ref[:, chunk(k)]
            one = decay_rows(dec_all, float(T))
            four = decay_rows(dec_all, float(4 * T))
            run = jnp.zeros((modes, ck), jnp.float32)
            far = run
            for zz in (range(Z) if w == 0 else range(Z - 1, -1, -1)):
                far = jnp.where(z == zz, run, far)
                run = four * run + pt[w, k // 4, zz]
            for c in (range(4) if w == 0 else range(3, -1, -1)):
                after = one * far + est[w, k // 4, c]
                est[w, k // 4, c] = far
                far = after
            entry[w, k] = est[w, k // 4, xc]
            for q in (1, 2, 3):
                enter_send(w, k, q).start()

    def second_pass(w, k, src, ring, slot, out):
        @pl.when(xc != owner(k))
        def _():
            enter_recv(w, k).wait_recv()
        entering = entry[w, k]
        row = lax.broadcasted_iota(jnp.int32, (8, 128), 0)
        seg = (row if w == 0 else 7 - row).astype(jnp.float32) * float(-L)
        for g in range(LG):
            dec = dec_ref[:, lanes(k, g)]
            res = res_ref[:, lanes(k, g)]
            init = []
            for m in range(modes):
                carried = entering[m:m + 1, g * 128:(g + 1) * 128]
                init.append(ring[slot, g, m] + jnp.exp(dec[m:m + 1] * seg) * carried)
            segment_run(src.at[slot, g], dec, res, init, out.at[g], L, w == 1)

    def fwd_first(k):
        load_x(k).wait()

        @pl.when(k + 1 < NK)
        def _():
            load_x(k + 1).start()
        slot = lax.rem(k, xs.shape[0])
        v = xin[lax.rem(k, xin.shape[0])].astype(jnp.float32)
        for g in range(LG):
            xs[slot, g] = v[:, g * 128:(g + 1) * 128]
        first_pass(0, k, xs, enf, slot)

    def fwd_second(k):
        second_pass(0, k, xs, enf, lax.rem(k, xs.shape[0]), conv.at[k])

    def back_first(k):
        psend(k).wait_recv()
        load_q(k).wait()

        @pl.when(k + 1 < NK)
        def _():
            load_q(k + 1).start()
        mixed = own[lax.rem(k, own.shape[0])] + pbuf[k]

        @pl.when(k >= 2)
        def _():
            store_q(k - 2).wait()
        slot = lax.rem(k, gs.shape[0])
        gate = qin[lax.rem(k, qin.shape[0])].astype(jnp.float32)
        for g in range(LG):
            sl = slice(g * 128, (g + 1) * 128)
            oq[lax.rem(k, 2), :, sl] = (mixed[:, sl] * conv[k, g]).astype(jnp.bfloat16)
            gs[slot, g] = mixed[:, sl] * gate[:, sl]
        store_q(k).start()
        first_pass(1, k, gs, enb, slot)

    def back_second(k):
        second_pass(1, k, gs, enb, lax.rem(k, gs.shape[0]), ys)

        @pl.when(k >= 2)
        def _():
            store_i(k - 2).wait()
        for g in range(LG):
            oi[lax.rem(k, 2), :, g * 128:(g + 1) * 128] = ys[g].astype(jnp.bfloat16)
        store_i(k).start()

    load_x(0).start()
    load_q(0).start()
    for zz in range(Z):
        @pl.when(zz > z)
        def _():
            pt[0, :, zz] = jnp.zeros((NK // 4, modes, ck), jnp.float32)

        @pl.when(zz < z)
        def _():
            pt[1, :, zz] = jnp.zeros((NK // 4, modes, ck), jnp.float32)

    def span(k, start, behind, f):
        def upto(t):
            return jnp.maximum(jnp.minimum(jnp.minimum(2 * (t - start + 1), t - behind + 1), NK), 0)

        def body(t, c):
            f(t)
            return c
        lax.fori_loop(upto(k - 1), upto(k), body, 0)

    def guard(k, f):
        @pl.when((k >= 0) & (k < NK))
        def _():
            f(k)

    def loop(k, c):
        guard(k, step_a)

        @pl.when(k == lag)
        def _():
            g_wait()
        span(k, lag, 2, matmul)
        guard(k, fwd_first)
        guard(k - 1, step_b)
        guard(k - 1, lambda t: middle(0, t))
        guard(k - 2, lambda t: late(0, t))
        guard(k - 3, fwd_second)
        span(k, lag + 1, 3, back_first)
        span(k, lag + 2, 4, lambda t: middle(1, t))
        span(k, lag + 3, 5, lambda t: late(1, t))
        span(k, lag + 4, 6, back_second)
        return c
    lax.fori_loop(0, NK + 6, loop, 0)

    def drain(k, c):
        @pl.when(k >= NK - NS)
        def _():
            psend(k).wait_send()

        @pl.when(k >= NK - 2)
        def _():
            store_q(k).wait()
            store_i(k).wait()
        zsend(k).wait_send()
        xfwd(k, 0).wait_send()
        xfwd(k, 1).wait_send()
        sib(k, 0).wait_send()
        sib(k, 1).wait_send()
        for w in range(2):
            @pl.when(xc != owner(k))
            def _():
                end_send(w, k).wait_send()

            @pl.when(xc == owner(k))
            def _():
                for q in (1, 2, 3):
                    enter_send(w, k, q).wait_send()
                for q in range(1, Z):
                    @pl.when(goes(w, q))
                    def _():
                        line_send(w, k, q).wait_send()
        return c
    lax.fori_loop(0, NK, drain, 0)
    for p in range(GP):
        def b():
            g_part(p).wait_send()

        def c():
            for d in range(1, C):
                g_own(p, d).wait_send()
                g_fwd(p, d).wait_send()
        guarded(other, b)
        guarded(mine, c)


def on_device(gated_input, query, out_grad, out_weight, decay_rate, residue, n, C,
              ck=256, GP=4, lag=4, win=2, pre=6, NS=4):
    T, fw = out_grad.shape
    cw, fb = out_weight.shape
    modes = decay_rate.shape[0]
    NK = cw // ck
    Z = n // 4
    lag = min(lag, NK - 1)
    split = n // C >= 8
    gcols, NG = (fw // 2, C) if split else (fw, C // 2)
    NS = min(NS, NK)
    LG = ck // 128
    cfg = (C, NK, ck, T, gcols, NG, fb, GP, lag, win, pre, NS, Z)
    S = pltpu.SemaphoreType.DMA
    bf, f32 = jnp.bfloat16, jnp.float32
    V = pltpu.VMEM
    any_spec = pl.BlockSpec(memory_space=pl.ANY)
    vmem_spec = pl.BlockSpec(memory_space=pltpu.VMEM)
    return pl.pallas_call(
        functools.partial(kernel, cfg),
        out_shape=(jax.ShapeDtypeStruct((T, cw), bf), jax.ShapeDtypeStruct((T, cw), bf)),
        in_specs=[any_spec] * 4 + [vmem_spec] * 2,
        out_specs=(any_spec, any_spec),
        scratch_shapes=[
            V((NK, 4, 2, ck, fb), bf),
            V((2, NG, T, gcols), bf),
            V((NK, T, ck), f32),
            V((NS, T, ck), f32),
            V((2 * T, ck), f32),
            V((6, T, ck), f32),
            V((NK, LG, T, 128), f32),
            V((2, T, ck), bf), V((2, T, ck), bf),
            V((4, LG, T, 128), f32), V((8, LG, T, 128), f32), V((LG, T, 128), f32),
            V((4, LG, modes, 8, 128), f32), V((8, LG, modes, 8, 128), f32),
            V((2, NK, modes, ck), f32), V((2, NK // 4, 4, modes, ck), f32),
            V((2, NK // 4, Z, modes, ck), f32), V((2, NK, modes, ck), f32),
            V((2, T, ck), bf), V((2, T, ck), bf),
            S((NK + 1,)),
            S((2, C, GP)), S((2, C, GP)),
            S((NK,)), S((NK,)),
            S((NK, 2)), S((NK, 2)),
            S((NK, 2)), S((NK, 2)),
            S((NK,)), S((NK,)),
            S((2, NK)), S((2, NK, 4)),
            S((2, NK, Z)), S((2, NK, Z)),
            S((2, NK, 4)), S((2, NK)),
            S((2,)), S((2,)), S((2,)), S((2,)),
        ],
        compiler_params=pltpu.CompilerParams(collective_id=0, has_side_effects=True, vmem_limit_bytes=60 * 1024 * 1024),
    )(out_grad, out_weight, gated_input, query, decay_rate, residue)


def solution(mesh):
    return jax.shard_map(
        functools.partial(on_device, n=mesh.shape["ctx"], C=mesh.shape["chan"]),
        mesh=mesh,
        in_specs=(
            P("ctx", "chan"),
            P("ctx", "chan"),
            P("ctx", "chan"),
            P("chan", "ctx"),
            P(None, "chan"),
            P(None, "chan"),
        ),
        out_specs=(P("ctx", "chan"), P("ctx", "chan")),
        check_vma=False,
    )
```

```python
import functools
import jax
import jax.numpy as jnp
from jax import lax
from jax.experimental import pallas as pl
from jax.experimental.pallas import tpu as pltpu
from jax.sharding import PartitionSpec as P

MESH = pl.DeviceIdType.MESH


def decay_rows(dec, scale):
    return jnp.exp(dec * (-scale))


LEVELS = 12
SPREAD = 20
STEP = 2.0 ** -7 / LEVELS
SHIFT = 100.0
PAD = 16


def encode(p, scale):
    v = p * (1.0 / scale)
    near = v.astype(jnp.bfloat16).astype(jnp.float32)
    small = jnp.abs(near) < 2.0 ** (1 - SPREAD)
    safe = jnp.where(small, 1.0, near)
    step = jnp.floor((v - near) / safe * (1.0 / STEP) + LEVELS / 2)
    step = jnp.minimum(jnp.maximum(step, 0.0), LEVELS - 1.0)
    return jnp.where(small, 0.0, near * jnp.exp2(step * SPREAD - SHIFT)).astype(jnp.bfloat16)


def decode(code, scale):
    y = code.astype(jnp.float32)
    power = jnp.log2(jnp.maximum(jnp.abs(y), 2.0 ** -120))
    step = jnp.floor((power + (SHIFT + SPREAD - 0.5)) * (1.0 / SPREAD))
    near = y * jnp.exp2(SHIFT - step * SPREAD)
    return near * (1.0 + (step + (0.5 - LEVELS / 2)) * STEP) * scale


def segment_run(src, dec, res, init, out, length, backward):
    modes = dec.shape[0]
    rate = jnp.exp(-dec)
    rates = [jnp.broadcast_to(rate[m:m + 1], (8, 128)) for m in range(modes)]
    if out is not None:
        gains = [jnp.broadcast_to(res[m:m + 1], (8, 128)) for m in range(modes)]
    unroll = 4

    def body(t, states):
        states = list(states)
        for u in range(unroll):
            tau = t * unroll + u
            if backward:
                tau = length - 1 - tau
            x = src[pl.ds(tau, 8, stride=length), :]
            states = [rates[m] * states[m] + x for m in range(modes)]
            if out is not None:
                terms = [gains[m] * states[m] for m in range(modes)]
                while len(terms) > 1:
                    terms = [terms[q] + terms[q + 1] for q in range(0, len(terms), 2)]
                out[pl.ds(tau, 8, stride=length), :] = terms[0]
        return tuple(states)

    return lax.fori_loop(0, length // unroll, body, tuple(init))


def segment_combine(ends, dec, length, backward):
    row = lax.broadcasted_iota(jnp.int32, (8, 128), 0)
    powers = [decay_rows(dec, float(length * sh)) for sh in (1, 2, 4)]
    enter, total = [], []
    for m, state in enumerate(ends):
        for sh, power in zip((1, 2, 4), powers):
            if backward:
                moved = jnp.where(row < 8 - sh, pltpu.roll(state, 8 - sh, 0), 0.0)
            else:
                moved = jnp.where(row >= sh, pltpu.roll(state, sh, 0), 0.0)
            state = state + power[m:m + 1] * moved
        if backward:
            enter.append(jnp.where(row < 7, pltpu.roll(state, 7, 0), 0.0))
            total.append(state[0:1])
        else:
            enter.append(jnp.where(row >= 1, pltpu.roll(state, 1, 0), 0.0))
            total.append(state[7:8])
    return enter, total


def kernel(cfg, g_ref, w_ref, x_ref, q_ref, dec_ref, res_ref, gq_ref, gi_ref,
           wbuf, gbuf, pbuf, gsend, acc, own, conv, xin, qin, xs, gs, ys, enf, enb, ends, est, pt, entry, oq, oi,
           l_s, g_s, g_r, z_s, z_r, x_s, x_r, s_s, s_r, m_s, m_r, e_s, e_r, t_s, t_r, o_s, o_r, xi_s, qi_s, oq_s, oi_s):
    C, NK, ck, T, gcols, NG, fb, GP, lag, win, pre, NS, Z = cfg
    L = T // 8
    LG = ck // 128
    modes = dec_ref.shape[0]
    z = lax.axis_index("ctx") // 4
    i = lax.axis_index("ctx")
    j = lax.axis_index("chan")
    zhi = i // 8
    zlo = lax.rem(i // 4, 2)
    xc = lax.rem(i, 4)
    ix = jnp.bitwise_xor(i, 2)
    isib = jnp.bitwise_xor(i, 1)
    iz = jnp.bitwise_xor(i, 8)
    ip = jnp.bitwise_xor(i, 4)

    def remote(src, dst, ss, rs, dev):
        return pltpu.make_async_remote_copy(src_ref=src, dst_ref=dst, send_sem=ss, recv_sem=rs, device_id=dev, device_id_type=MESH)

    barrier = pltpu.get_barrier_semaphore()
    peers = [(jnp.bitwise_xor(i, q), j) for q in (1, 2, 3)]
    peers += [(jnp.bitwise_xor(z, q) * 4 + xc, j) for q in range(1, Z)]
    peers += [(i, lax.rem(j + d, C)) for d in range(1, C)]
    for dev in peers:
        pl.semaphore_signal(barrier, inc=1, device_id=dev, device_id_type=MESH)
    pl.semaphore_wait(barrier, len(peers))

    rp = T // GP
    split = NG == C

    def slot_of(jj):
        return jj if split else (jj // (2 * (NG // 2))) * (NG // 2) + lax.rem(jj, NG // 2)

    def active(jj, half):
        return None if split else lax.rem(jj // (NG // 2), 2) == half

    def guarded(cond, f):
        if cond is None:
            f()
        else:
            pl.when(cond)(f)

    def cols(half):
        return pl.ds(pl.multiple_of(half * gcols, gcols), gcols) if split else pl.ds(0, gcols)

    def rows(p):
        return pl.ds(p * rp, rp)

    def peer(d):
        return (i, lax.rem(j + d, C))

    me_slot = slot_of(j)

    def g_own(p, d):
        return remote(g_ref.at[rows(p), cols(zlo)], gbuf.at[0, me_slot, rows(p), :], g_s.at[0, d, p], g_r.at[0, d, p], peer(d))

    def g_part(p):
        return remote(g_ref.at[rows(p), cols(1 - zlo)], gbuf.at[1, me_slot, rows(p), :], g_s.at[1, 0, p], g_r.at[1, 0, p], (ip, j))

    def g_fwd(p, d):
        return remote(gbuf.at[1, me_slot, rows(p), :], gbuf.at[1, me_slot, rows(p), :], g_s.at[1, d, p], g_r.at[1, d, p], peer(d))

    def g_local():
        return pltpu.make_async_copy(g_ref.at[:, cols(zlo)], gbuf.at[0, me_slot], l_s.at[0])

    def wrows(k):
        return w_ref.at[pl.ds(pl.multiple_of(k * ck, ck), ck), :]

    def wlocal(k):
        return pltpu.make_async_copy(wrows(k), wbuf.at[k, xc, zhi], l_s.at[k + 1])

    def zsend(k):
        return remote(wrows(k), wbuf.at[k, xc, zhi], z_s.at[k], z_r.at[k], (iz, j))

    def zrecv(k):
        return remote(wrows(k), wbuf.at[k, xc, 1 - zhi], z_s.at[k], z_r.at[k], (iz, j))

    def xfwd(k, b):
        zz = zhi if b == 0 else 1 - zhi
        return remote(wbuf.at[k, xc, zz], wbuf.at[k, xc, zz], x_s.at[k, b], x_r.at[k, b], (ix, j))

    def xrecv(k, b):
        zz = zhi if b == 0 else 1 - zhi
        s = jnp.bitwise_xor(xc, 2)
        return remote(wbuf.at[k, s, zz], wbuf.at[k, s, zz], x_s.at[k, b], x_r.at[k, b], (ix, j))

    def sib(k, b):
        s = jnp.bitwise_xor(xc, 2 * b)
        return remote(wbuf.at[k, s], wbuf.at[k, s], s_s.at[k, b], s_r.at[k, b], (isib, j))

    def sibrecv(k, b):
        s = jnp.bitwise_xor(xc, 2 * b + 1)
        return remote(wbuf.at[k, s], wbuf.at[k, s], s_s.at[k, b], s_r.at[k, b], (isib, j))

    def psend(k):
        return remote(gsend.at[lax.rem(k, NS)], pbuf.at[k], m_s.at[k], m_r.at[k], (ip, j))

    mine = active(j, zlo)
    other = active(j, 1 - zlo)

    def start_g():
        def a():
            g_local().start()
        guarded(mine, a)
        for p in range(GP):
            def b():
                g_part(p).start()

            def c():
                for d in range(1, C):
                    g_own(p, d).start()
            guarded(other, b)
            guarded(mine, c)

    start_g()
    for k in range(NK):
        wlocal(k).start()
    for k in range(min(win, NK)):
        zsend(k).start()
    for k in range(min(pre, NK)):
        wlocal(k).wait()
        xfwd(k, 0).start()

    def fwd_g():
        for p in range(GP):
            g_part(p).wait_recv()
            for d in range(1, C):
                g_fwd(p, d).start()
    guarded(mine, fwd_g)

    def g_wait():
        def a():
            g_local().wait()
        guarded(mine, a)
        for d in range(1, C):
            jj = lax.rem(j + C - d, C)
            sl = slot_of(jj)

            def b():
                for p in range(GP):
                    for h in range(2):
                        r = gbuf.at[h, sl, rows(p), :]
                        remote(r, r, g_s.at[h, d, p], g_r.at[h, d, p], (i, jj)).wait_recv()
            guarded(active(jj, zlo), b)

    per = gcols // fb

    def matmul(k):
        sibrecv(k, 0).wait_recv()
        sibrecv(k, 1).wait_recv()

        for u in range(8):
            a = gbuf[:, u // per, :, (u % per) * fb:(u % per + 1) * fb].reshape(2 * T, fb)
            b = wbuf[k, u % 4, u // 4]
            r = lax.dot_general(a, b, (((1,), (1,)), ((), ())), preferred_element_type=jnp.float32)
            if u == 0:
                acc[...] = r
            else:
                acc[...] += r

        @pl.when(k >= NS)
        def _():
            psend(k - NS).wait_send()
        own[lax.rem(k, own.shape[0])] = acc[0:T, :]
        slot = lax.rem(k, NS)
        top = jnp.max(jnp.abs(acc[T:2 * T, :]), axis=0, keepdims=True)
        scale = (jnp.maximum(top, 1e-30) * 1.008).astype(jnp.bfloat16)
        gsend[slot, T:T + PAD, :] = jnp.broadcast_to(scale, (PAD, ck))
        scale = scale.astype(jnp.float32)

        def pack(b, c):
            at = pl.multiple_of(b * 32, 32)
            gsend[slot, pl.ds(at, 32), :] = encode(acc[pl.ds(pl.multiple_of(T + at, 32), 32), :], scale)
            return c
        lax.fori_loop(0, T // 32, pack, 0)
        psend(k).start()

    def step_a(k):
        @pl.when(k + pre < NK)
        def _():
            wlocal(k + pre).wait()
            xfwd(k + pre, 0).start()
        zrecv(k).wait_recv()
        xfwd(k, 1).start()
        sib(k, 0).start()

        @pl.when(k + win < NK)
        def _():
            zsend(k + win).start()

    def step_b(k):
        for b in range(2):
            xrecv(k, b).wait_recv()
        sib(k, 1).start()

    def lanes(k, g):
        return pl.ds(pl.multiple_of(k * ck + g * 128, 128), 128)

    def chunk(k):
        return pl.ds(pl.multiple_of(k * ck, ck), ck)

    def load_x(k):
        sl = lax.rem(k, xin.shape[0])
        return pltpu.make_async_copy(x_ref.at[:, chunk(k)], xin.at[sl], xi_s.at[sl])

    def load_q(k):
        sl = lax.rem(k, qin.shape[0])
        return pltpu.make_async_copy(q_ref.at[:, chunk(k)], qin.at[sl], qi_s.at[sl])

    def store_q(k):
        sl = lax.rem(k, 2)
        return pltpu.make_async_copy(oq.at[sl], gq_ref.at[:, chunk(k)], oq_s.at[sl])

    def store_i(k):
        sl = lax.rem(k, 2)
        return pltpu.make_async_copy(oi.at[sl], gi_ref.at[:, chunk(k)], oi_s.at[sl])

    def owner(k):
        return lax.rem(k, 4)

    def end_send(w, k):
        return remote(ends.at[w, k], est.at[w, k // 4, xc], e_s.at[w, k], e_r.at[w, k, xc], (z * 4 + owner(k), j))

    def end_recv(w, k, q):
        c = jnp.bitwise_xor(xc, q)
        return remote(ends.at[w, k], est.at[w, k // 4, c], e_s.at[w, k], e_r.at[w, k, c], (z * 4 + c, j))

    def line_send(w, k, q):
        r = pt.at[w, k // 4, z]
        return remote(r, r, t_s.at[w, k, q], t_r.at[w, k, q], (jnp.bitwise_xor(z, q) * 4 + xc, j))

    def line_recv(w, k, q):
        zz = jnp.bitwise_xor(z, q)
        r = pt.at[w, k // 4, zz]
        return remote(r, r, t_s.at[w, k, q], t_r.at[w, k, q], (zz * 4 + xc, j))

    def enter_send(w, k, q):
        c = jnp.bitwise_xor(xc, q)
        return remote(est.at[w, k // 4, c], entry.at[w, k], o_s.at[w, k, q], o_r.at[w, k], (z * 4 + c, j))

    def enter_recv(w, k):
        return remote(ends.at[w, k], entry.at[w, k], e_s.at[w, k], o_r.at[w, k], (z * 4 + owner(k), j))

    def goes(w, q):
        zz = jnp.bitwise_xor(z, q)
        return zz > z if w == 0 else zz < z

    def comes(w, q):
        zz = jnp.bitwise_xor(z, q)
        return zz < z if w == 0 else zz > z

    def first_pass(w, k, src, ring, slot):
        for g in range(LG):
            dec = dec_ref[:, lanes(k, g)]
            zero = [jnp.zeros((8, 128), jnp.float32)] * modes
            outs = segment_run(src.at[slot, g], dec, None, zero, None, L, w == 1)
            enter, total = segment_combine(outs, dec, L, w == 1)
            for m in range(modes):
                ring[slot, g, m] = enter[m]
                ends[w, k, m:m + 1, g * 128:(g + 1) * 128] = total[m]

        @pl.when(xc == owner(k))
        def _():
            est[w, k // 4, xc] = ends[w, k]

        @pl.when(xc != owner(k))
        def _():
            end_send(w, k).start()

    def middle(w, k):
        @pl.when(xc == owner(k))
        def _():
            for q in (1, 2, 3):
                end_recv(w, k, q).wait_recv()
            one = decay_rows(dec_ref[:, chunk(k)], float(T))
            run = jnp.zeros((modes, ck), jnp.float32)
            for c in (range(4) if w == 0 else range(3, -1, -1)):
                run = one * run + est[w, k // 4, c]
            pt[w, k // 4, z] = run
            for q in range(1, Z):
                @pl.when(goes(w, q))
                def _():
                    line_send(w, k, q).start()

    def late(w, k):
        @pl.when(xc == owner(k))
        def _():
            for q in range(1, Z):
                @pl.when(comes(w, q))
                def _():
                    line_recv(w, k, q).wait_recv()
            dec_all = dec_ref[:, chunk(k)]
            one = decay_rows(dec_all, float(T))
            four = decay_rows(dec_all, float(4 * T))
            run = jnp.zeros((modes, ck), jnp.float32)
            far = run
            for zz in (range(Z) if w == 0 else range(Z - 1, -1, -1)):
                far = jnp.where(z == zz, run, far)
                run = four * run + pt[w, k // 4, zz]
            for c in (range(4) if w == 0 else range(3, -1, -1)):
                after = one * far + est[w, k // 4, c]
                est[w, k // 4, c] = far
                far = after
            entry[w, k] = est[w, k // 4, xc]
            for q in (1, 2, 3):
                enter_send(w, k, q).start()

    def second_pass(w, k, src, ring, slot, out):
        @pl.when(xc != owner(k))
        def _():
            enter_recv(w, k).wait_recv()
        entering = entry[w, k]
        row = lax.broadcasted_iota(jnp.int32, (8, 128), 0)
        seg = (row if w == 0 else 7 - row).astype(jnp.float32) * float(-L)
        for g in range(LG):
            dec = dec_ref[:, lanes(k, g)]
            res = res_ref[:, lanes(k, g)]
            init = []
            for m in range(modes):
                carried = entering[m:m + 1, g * 128:(g + 1) * 128]
                init.append(ring[slot, g, m] + jnp.exp(dec[m:m + 1] * seg) * carried)
            segment_run(src.at[slot, g], dec, res, init, out.at[g], L, w == 1)

    def fwd_first(k):
        load_x(k).wait()

        @pl.when(k + 1 < NK)
        def _():
            load_x(k + 1).start()
        slot = lax.rem(k, xs.shape[0])
        v = xin[lax.rem(k, xin.shape[0])].astype(jnp.float32)
        for g in range(LG):
            xs[slot, g] = v[:, g * 128:(g + 1) * 128]
        first_pass(0, k, xs, enf, slot)

    def fwd_second(k):
        second_pass(0, k, xs, enf, lax.rem(k, xs.shape[0]), conv.at[k])

    def back_first(k):
        psend(k).wait_recv()
        load_q(k).wait()

        @pl.when(k + 1 < NK)
        def _():
            load_q(k + 1).start()
        @pl.when(k >= 2)
        def _():
            store_q(k - 2).wait()
        slot = lax.rem(k, gs.shape[0])
        scale = pbuf[k, T:T + PAD, :].astype(jnp.float32)[0:1]

        def gates(b, c):
            r = pl.ds(pl.multiple_of(b * 32, 32), 32)
            mixed = own[lax.rem(k, own.shape[0]), r, :] + decode(pbuf[k, r, :], scale)
            gate = qin[lax.rem(k, qin.shape[0]), r, :].astype(jnp.float32)
            for g in range(LG):
                sl = slice(g * 128, (g + 1) * 128)
                oq[lax.rem(k, 2), r, sl] = (mixed[:, sl] * conv[k, g, r, :]).astype(jnp.bfloat16)
                gs[slot, g, r, :] = mixed[:, sl] * gate[:, sl]
            return c
        lax.fori_loop(0, T // 32, gates, 0)
        store_q(k).start()
        first_pass(1, k, gs, enb, slot)

    def back_second(k):
        second_pass(1, k, gs, enb, lax.rem(k, gs.shape[0]), ys)

        @pl.when(k >= 2)
        def _():
            store_i(k - 2).wait()
        for g in range(LG):
            oi[lax.rem(k, 2), :, g * 128:(g + 1) * 128] = ys[g].astype(jnp.bfloat16)
        store_i(k).start()

    load_x(0).start()
    load_q(0).start()
    for zz in range(Z):
        @pl.when(zz > z)
        def _():
            pt[0, :, zz] = jnp.zeros((NK // 4, modes, ck), jnp.float32)

        @pl.when(zz < z)
        def _():
            pt[1, :, zz] = jnp.zeros((NK // 4, modes, ck), jnp.float32)

    def span(k, start, behind, f):
        def upto(t):
            return jnp.maximum(jnp.minimum(jnp.minimum(2 * (t - start + 1), t - behind + 1), NK), 0)

        def body(t, c):
            f(t)
            return c
        lax.fori_loop(upto(k - 1), upto(k), body, 0)

    def guard(k, f):
        @pl.when((k >= 0) & (k < NK))
        def _():
            f(k)

    def loop(k, c):
        guard(k, step_a)

        @pl.when(k == lag)
        def _():
            g_wait()
        span(k, lag, 2, matmul)
        guard(k, fwd_first)
        guard(k - 1, step_b)
        guard(k - 1, lambda t: middle(0, t))
        guard(k - 2, lambda t: late(0, t))
        guard(k - 3, fwd_second)
        span(k, lag + 1, 3, back_first)
        span(k, lag + 2, 4, lambda t: middle(1, t))
        span(k, lag + 3, 5, lambda t: late(1, t))
        span(k, lag + 4, 6, back_second)
        return c
    lax.fori_loop(0, NK + 6, loop, 0)

    def drain(k, c):
        @pl.when(k >= NK - NS)
        def _():
            psend(k).wait_send()

        @pl.when(k >= NK - 2)
        def _():
            store_q(k).wait()
            store_i(k).wait()
        zsend(k).wait_send()
        xfwd(k, 0).wait_send()
        xfwd(k, 1).wait_send()
        sib(k, 0).wait_send()
        sib(k, 1).wait_send()
        for w in range(2):
            @pl.when(xc != owner(k))
            def _():
                end_send(w, k).wait_send()

            @pl.when(xc == owner(k))
            def _():
                for q in (1, 2, 3):
                    enter_send(w, k, q).wait_send()
                for q in range(1, Z):
                    @pl.when(goes(w, q))
                    def _():
                        line_send(w, k, q).wait_send()
        return c
    lax.fori_loop(0, NK, drain, 0)
    for p in range(GP):
        def b():
            g_part(p).wait_send()

        def c():
            for d in range(1, C):
                g_own(p, d).wait_send()
                g_fwd(p, d).wait_send()
        guarded(other, b)
        guarded(mine, c)


def on_device(gated_input, query, out_grad, out_weight, decay_rate, residue, n, C,
              ck=256, GP=4, lag=4, win=2, pre=4, NS=4):
    T, fw = out_grad.shape
    cw, fb = out_weight.shape
    modes = decay_rate.shape[0]
    NK = cw // ck
    Z = n // 4
    lag = min(lag, NK - 1)
    split = n // C >= 8
    gcols, NG = (fw // 2, C) if split else (fw, C // 2)
    NS = min(NS, NK)
    LG = ck // 128
    cfg = (C, NK, ck, T, gcols, NG, fb, GP, lag, win, pre, NS, Z)
    S = pltpu.SemaphoreType.DMA
    bf, f32 = jnp.bfloat16, jnp.float32
    V = pltpu.VMEM
    any_spec = pl.BlockSpec(memory_space=pl.ANY)
    vmem_spec = pl.BlockSpec(memory_space=pltpu.VMEM)
    return pl.pallas_call(
        functools.partial(kernel, cfg),
        out_shape=(jax.ShapeDtypeStruct((T, cw), bf), jax.ShapeDtypeStruct((T, cw), bf)),
        in_specs=[any_spec] * 4 + [vmem_spec] * 2,
        out_specs=(any_spec, any_spec),
        scratch_shapes=[
            V((NK, 4, 2, ck, fb), bf),
            V((2, NG, T, gcols), bf),
            V((NK, T + PAD, ck), bf),
            V((NS, T + PAD, ck), bf),
            V((2 * T, ck), f32),
            V((6, T, ck), f32),
            V((NK, LG, T, 128), f32),
            V((2, T, ck), bf), V((2, T, ck), bf),
            V((4, LG, T, 128), f32), V((8, LG, T, 128), f32), V((LG, T, 128), f32),
            V((4, LG, modes, 8, 128), f32), V((8, LG, modes, 8, 128), f32),
            V((2, NK, modes, ck), f32), V((2, NK // 4, 4, modes, ck), f32),
            V((2, NK // 4, Z, modes, ck), f32), V((2, NK, modes, ck), f32),
            V((2, T, ck), bf), V((2, T, ck), bf),
            S((NK + 1,)),
            S((2, C, GP)), S((2, C, GP)),
            S((NK,)), S((NK,)),
            S((NK, 2)), S((NK, 2)),
            S((NK, 2)), S((NK, 2)),
            S((NK,)), S((NK,)),
            S((2, NK)), S((2, NK, 4)),
            S((2, NK, Z)), S((2, NK, Z)),
            S((2, NK, 4)), S((2, NK)),
            S((2,)), S((2,)), S((2,)), S((2,)),
        ],
        compiler_params=pltpu.CompilerParams(collective_id=0, has_side_effects=True, vmem_limit_bytes=60 * 1024 * 1024),
    )(out_grad, out_weight, gated_input, query, decay_rate, residue)


def solution(mesh):
    return jax.shard_map(
        functools.partial(on_device, n=mesh.shape["ctx"], C=mesh.shape["chan"]),
        mesh=mesh,
        in_specs=(
            P("ctx", "chan"),
            P("ctx", "chan"),
            P("ctx", "chan"),
            P("chan", "ctx"),
            P(None, "chan"),
            P(None, "chan"),
        ),
        out_specs=(P("ctx", "chan"), P("ctx", "chan")),
        check_vma=False,
    )
```

```python
import functools
import jax
import jax.numpy as jnp
from jax import lax
from jax.experimental import pallas as pl
from jax.experimental.pallas import tpu as pltpu
from jax.sharding import PartitionSpec as P

MESH = pl.DeviceIdType.MESH


def decay_rows(dec, scale):
    return jnp.exp(dec * (-scale))


LEVELS = 12
SPREAD = 20
STEP = 2.0 ** -7 / LEVELS
SHIFT = 100.0
PAD = 16


def encode(p, scale):
    v = p * (1.0 / scale)
    near = v.astype(jnp.bfloat16).astype(jnp.float32)
    small = jnp.abs(near) < 2.0 ** (1 - SPREAD)
    safe = jnp.where(small, 1.0, near)
    step = jnp.floor((v - near) / safe * (1.0 / STEP) + LEVELS / 2)
    step = jnp.minimum(jnp.maximum(step, 0.0), LEVELS - 1.0)
    return jnp.where(small, 0.0, near * jnp.exp2(step * SPREAD - SHIFT)).astype(jnp.bfloat16)


def decode(code, scale):
    y = code.astype(jnp.float32)
    power = jnp.log2(jnp.maximum(jnp.abs(y), 2.0 ** -120))
    step = jnp.floor((power + (SHIFT + SPREAD - 0.5)) * (1.0 / SPREAD))
    near = y * jnp.exp2(SHIFT - step * SPREAD)
    return near * (1.0 + (step + (0.5 - LEVELS / 2)) * STEP) * scale


def segment_run(src, dec, res, init, out, length, backward):
    modes = dec.shape[0]
    rate = jnp.exp(-dec)
    rates = [jnp.broadcast_to(rate[m:m + 1], (8, 128)) for m in range(modes)]
    if out is not None:
        gains = [jnp.broadcast_to(res[m:m + 1], (8, 128)) for m in range(modes)]
    unroll = 4

    def body(t, states):
        states = list(states)
        for u in range(unroll):
            tau = t * unroll + u
            if backward:
                tau = length - 1 - tau
            x = src[pl.ds(tau, 8, stride=length), :]
            states = [rates[m] * states[m] + x for m in range(modes)]
            if out is not None:
                terms = [gains[m] * states[m] for m in range(modes)]
                while len(terms) > 1:
                    terms = [terms[q] + terms[q + 1] for q in range(0, len(terms), 2)]
                out[pl.ds(tau, 8, stride=length), :] = terms[0]
        return tuple(states)

    return lax.fori_loop(0, length // unroll, body, tuple(init))


def segment_combine(ends, dec, length, backward):
    row = lax.broadcasted_iota(jnp.int32, (8, 128), 0)
    powers = [decay_rows(dec, float(length * sh)) for sh in (1, 2, 4)]
    enter, total = [], []
    for m, state in enumerate(ends):
        for sh, power in zip((1, 2, 4), powers):
            if backward:
                moved = jnp.where(row < 8 - sh, pltpu.roll(state, 8 - sh, 0), 0.0)
            else:
                moved = jnp.where(row >= sh, pltpu.roll(state, sh, 0), 0.0)
            state = state + power[m:m + 1] * moved
        if backward:
            enter.append(jnp.where(row < 7, pltpu.roll(state, 7, 0), 0.0))
            total.append(state[0:1])
        else:
            enter.append(jnp.where(row >= 1, pltpu.roll(state, 1, 0), 0.0))
            total.append(state[7:8])
    return enter, total


def kernel(cfg, g_ref, w_ref, x_ref, q_ref, dec_ref, res_ref, gq_ref, gi_ref,
           wbuf, gbuf, pbuf, gsend, acc, own, conv, xin, qin, xs, gs, ys, enf, enb, ends, est, pt, entry, est_last, pt_last, oq, oi,
           l_s, g_s, g_r, z_s, z_r, x_s, x_r, s_s, s_r, m_s, m_r, e_s, e_r, t_s, t_r, o_s, o_r, ls_s, ls_r, lt_s, lt_r, xi_s, qi_s, oq_s, oi_s):
    C, NK, ck, T, gcols, NG, fb, GP, lag, win, pre, NS, Z = cfg
    L = T // 8
    LG = ck // 128
    modes = dec_ref.shape[0]
    z = lax.axis_index("ctx") // 4
    i = lax.axis_index("ctx")
    j = lax.axis_index("chan")
    zhi = i // 8
    zlo = lax.rem(i // 4, 2)
    xc = lax.rem(i, 4)
    ix = jnp.bitwise_xor(i, 2)
    isib = jnp.bitwise_xor(i, 1)
    iz = jnp.bitwise_xor(i, 8)
    ip = jnp.bitwise_xor(i, 4)

    def remote(src, dst, ss, rs, dev):
        return pltpu.make_async_remote_copy(src_ref=src, dst_ref=dst, send_sem=ss, recv_sem=rs, device_id=dev, device_id_type=MESH)

    barrier = pltpu.get_barrier_semaphore()
    peers = [(jnp.bitwise_xor(i, q), j) for q in (1, 2, 3)]
    peers += [(jnp.bitwise_xor(z, q) * 4 + xc, j) for q in range(1, Z)]
    peers += [(i, lax.rem(j + d, C)) for d in range(1, C)]
    for dev in peers:
        pl.semaphore_signal(barrier, inc=1, device_id=dev, device_id_type=MESH)
    pl.semaphore_wait(barrier, len(peers))

    rp = T // GP
    split = NG == C

    def slot_of(jj):
        return jj if split else (jj // (2 * (NG // 2))) * (NG // 2) + lax.rem(jj, NG // 2)

    def active(jj, half):
        return None if split else lax.rem(jj // (NG // 2), 2) == half

    def guarded(cond, f):
        if cond is None:
            f()
        else:
            pl.when(cond)(f)

    def cols(half):
        return pl.ds(pl.multiple_of(half * gcols, gcols), gcols) if split else pl.ds(0, gcols)

    def rows(p):
        return pl.ds(p * rp, rp)

    def peer(d):
        return (i, lax.rem(j + d, C))

    me_slot = slot_of(j)

    def g_own(p, d):
        return remote(g_ref.at[rows(p), cols(zlo)], gbuf.at[0, me_slot, rows(p), :], g_s.at[0, d, p], g_r.at[0, d, p], peer(d))

    def g_part(p):
        return remote(g_ref.at[rows(p), cols(1 - zlo)], gbuf.at[1, me_slot, rows(p), :], g_s.at[1, 0, p], g_r.at[1, 0, p], (ip, j))

    def g_fwd(p, d):
        return remote(gbuf.at[1, me_slot, rows(p), :], gbuf.at[1, me_slot, rows(p), :], g_s.at[1, d, p], g_r.at[1, d, p], peer(d))

    def g_local():
        return pltpu.make_async_copy(g_ref.at[:, cols(zlo)], gbuf.at[0, me_slot], l_s.at[0])

    def wrows(k):
        return w_ref.at[pl.ds(pl.multiple_of(k * ck, ck), ck), :]

    def wlocal(k):
        return pltpu.make_async_copy(wrows(k), wbuf.at[k, xc, zhi], l_s.at[k + 1])

    def zsend(k):
        return remote(wrows(k), wbuf.at[k, xc, zhi], z_s.at[k], z_r.at[k], (iz, j))

    def zrecv(k):
        return remote(wrows(k), wbuf.at[k, xc, 1 - zhi], z_s.at[k], z_r.at[k], (iz, j))

    def xfwd(k, b):
        zz = zhi if b == 0 else 1 - zhi
        return remote(wbuf.at[k, xc, zz], wbuf.at[k, xc, zz], x_s.at[k, b], x_r.at[k, b], (ix, j))

    def xrecv(k, b):
        zz = zhi if b == 0 else 1 - zhi
        s = jnp.bitwise_xor(xc, 2)
        return remote(wbuf.at[k, s, zz], wbuf.at[k, s, zz], x_s.at[k, b], x_r.at[k, b], (ix, j))

    def sib(k, b):
        s = jnp.bitwise_xor(xc, 2 * b)
        return remote(wbuf.at[k, s], wbuf.at[k, s], s_s.at[k, b], s_r.at[k, b], (isib, j))

    def sibrecv(k, b):
        s = jnp.bitwise_xor(xc, 2 * b + 1)
        return remote(wbuf.at[k, s], wbuf.at[k, s], s_s.at[k, b], s_r.at[k, b], (isib, j))

    def psend(k):
        return remote(gsend.at[lax.rem(k, NS)], pbuf.at[k], m_s.at[k], m_r.at[k], (ip, j))

    mine = active(j, zlo)
    other = active(j, 1 - zlo)

    def start_g():
        def a():
            g_local().start()
        guarded(mine, a)
        for p in range(GP):
            def b():
                g_part(p).start()

            def c():
                for d in range(1, C):
                    g_own(p, d).start()
            guarded(other, b)
            guarded(mine, c)

    start_g()
    for k in range(NK):
        wlocal(k).start()
    for k in range(min(win, NK)):
        zsend(k).start()
    for k in range(min(pre, NK)):
        wlocal(k).wait()
        xfwd(k, 0).start()

    def fwd_g():
        for p in range(GP):
            g_part(p).wait_recv()
            for d in range(1, C):
                g_fwd(p, d).start()
    guarded(mine, fwd_g)

    def g_wait():
        def a():
            g_local().wait()
        guarded(mine, a)
        for d in range(1, C):
            jj = lax.rem(j + C - d, C)
            sl = slot_of(jj)

            def b():
                for p in range(GP):
                    for h in range(2):
                        r = gbuf.at[h, sl, rows(p), :]
                        remote(r, r, g_s.at[h, d, p], g_r.at[h, d, p], (i, jj)).wait_recv()
            guarded(active(jj, zlo), b)

    per = gcols // fb

    def matmul(k):
        sibrecv(k, 0).wait_recv()
        sibrecv(k, 1).wait_recv()

        for u in range(8):
            a = gbuf[:, u // per, :, (u % per) * fb:(u % per + 1) * fb].reshape(2 * T, fb)
            b = wbuf[k, u % 4, u // 4]
            r = lax.dot_general(a, b, (((1,), (1,)), ((), ())), preferred_element_type=jnp.float32)
            if u == 0:
                acc[...] = r
            else:
                acc[...] += r

        @pl.when(k >= NS)
        def _():
            psend(k - NS).wait_send()
        own[lax.rem(k, own.shape[0])] = acc[0:T, :]
        slot = lax.rem(k, NS)
        top = jnp.max(jnp.abs(acc[T:2 * T, :]), axis=0, keepdims=True)
        scale = (jnp.maximum(top, 1e-30) * 1.008).astype(jnp.bfloat16)
        gsend[slot, T:T + PAD, :] = jnp.broadcast_to(scale, (PAD, ck))
        scale = scale.astype(jnp.float32)

        def pack(b, c):
            at = pl.multiple_of(b * 32, 32)
            gsend[slot, pl.ds(at, 32), :] = encode(acc[pl.ds(pl.multiple_of(T + at, 32), 32), :], scale)
            return c
        lax.fori_loop(0, T // 32, pack, 0)
        psend(k).start()

    def step_a(k):
        @pl.when(k + pre < NK)
        def _():
            wlocal(k + pre).wait()
            xfwd(k + pre, 0).start()
        zrecv(k).wait_recv()
        xfwd(k, 1).start()
        sib(k, 0).start()

        @pl.when(k + win < NK)
        def _():
            zsend(k + win).start()

    def step_b(k):
        for b in range(2):
            xrecv(k, b).wait_recv()
        sib(k, 1).start()

    def lanes(k, g):
        return pl.ds(pl.multiple_of(k * ck + g * 128, 128), 128)

    def chunk(k):
        return pl.ds(pl.multiple_of(k * ck, ck), ck)

    def load_x(k):
        sl = lax.rem(k, xin.shape[0])
        return pltpu.make_async_copy(x_ref.at[:, chunk(k)], xin.at[sl], xi_s.at[sl])

    def load_q(k):
        sl = lax.rem(k, qin.shape[0])
        return pltpu.make_async_copy(q_ref.at[:, chunk(k)], qin.at[sl], qi_s.at[sl])

    def store_q(k):
        sl = lax.rem(k, 2)
        return pltpu.make_async_copy(oq.at[sl], gq_ref.at[:, chunk(k)], oq_s.at[sl])

    def store_i(k):
        sl = lax.rem(k, 2)
        return pltpu.make_async_copy(oi.at[sl], gi_ref.at[:, chunk(k)], oi_s.at[sl])

    def owner(k):
        return lax.rem(k, 4)

    def end_send(w, k):
        return remote(ends.at[w, k], est.at[w, k // 4, xc], e_s.at[w, k], e_r.at[w, k, xc], (z * 4 + owner(k), j))

    def end_recv(w, k, q):
        c = jnp.bitwise_xor(xc, q)
        return remote(ends.at[w, k], est.at[w, k // 4, c], e_s.at[w, k], e_r.at[w, k, c], (z * 4 + c, j))

    def line_send(w, k, q):
        r = pt.at[w, k // 4, z]
        return remote(r, r, t_s.at[w, k, q], t_r.at[w, k, q], (jnp.bitwise_xor(z, q) * 4 + xc, j))

    def line_recv(w, k, q):
        zz = jnp.bitwise_xor(z, q)
        r = pt.at[w, k // 4, zz]
        return remote(r, r, t_s.at[w, k, q], t_r.at[w, k, q], (zz * 4 + xc, j))

    def enter_send(w, k, q):
        c = jnp.bitwise_xor(xc, q)
        return remote(est.at[w, k // 4, c], entry.at[w, k], o_s.at[w, k, q], o_r.at[w, k], (z * 4 + c, j))

    def enter_recv(w, k):
        return remote(ends.at[w, k], entry.at[w, k], e_s.at[w, k], o_r.at[w, k], (z * 4 + owner(k), j))

    def last_send(q):
        return remote(est_last.at[xc], est_last.at[xc], ls_s.at[q], ls_r.at[q], (jnp.bitwise_xor(i, q), j))

    def last_recv(q):
        r = est_last.at[jnp.bitwise_xor(xc, q)]
        return remote(r, r, ls_s.at[q], ls_r.at[q], (jnp.bitwise_xor(i, q), j))

    def last_line_send(q):
        return remote(pt_last.at[z], pt_last.at[z], lt_s.at[q], lt_r.at[q], (jnp.bitwise_xor(z, q) * 4 + xc, j))

    def last_line_recv(q):
        zz = jnp.bitwise_xor(z, q)
        return remote(pt_last.at[zz], pt_last.at[zz], lt_s.at[q], lt_r.at[q], (zz * 4 + xc, j))

    LAST = NK - 1

    def goes(w, q):
        zz = jnp.bitwise_xor(z, q)
        return zz > z if w == 0 else zz < z

    def comes(w, q):
        zz = jnp.bitwise_xor(z, q)
        return zz < z if w == 0 else zz > z

    def first_pass(w, k, src, ring, slot):
        for g in range(LG):
            dec = dec_ref[:, lanes(k, g)]
            zero = [jnp.zeros((8, 128), jnp.float32)] * modes
            outs = segment_run(src.at[slot, g], dec, None, zero, None, L, w == 1)
            enter, total = segment_combine(outs, dec, L, w == 1)
            for m in range(modes):
                ring[slot, g, m] = enter[m]
                ends[w, k, m:m + 1, g * 128:(g + 1) * 128] = total[m]

        chained = True if w == 0 else k != LAST

        @pl.when((xc == owner(k)) & chained)
        def _():
            est[w, k // 4, xc] = ends[w, k]

        @pl.when((xc != owner(k)) & chained)
        def _():
            end_send(w, k).start()

        if w == 1:
            @pl.when(k == LAST)
            def _():
                est_last[xc] = ends[w, LAST]
                for q in (1, 2, 3):
                    last_send(q).start()

    def middle(w, k):
        @pl.when(xc == owner(k))
        def _():
            for q in (1, 2, 3):
                end_recv(w, k, q).wait_recv()
            one = decay_rows(dec_ref[:, chunk(k)], float(T))
            run = jnp.zeros((modes, ck), jnp.float32)
            for c in (range(4) if w == 0 else range(3, -1, -1)):
                run = one * run + est[w, k // 4, c]
            pt[w, k // 4, z] = run
            for q in range(1, Z):
                @pl.when(goes(w, q))
                def _():
                    line_send(w, k, q).start()

    def middle_last():
        for q in (1, 2, 3):
            last_recv(q).wait_recv()
        one = decay_rows(dec_ref[:, chunk(LAST)], float(T))
        run = jnp.zeros((modes, ck), jnp.float32)
        for c in range(3, -1, -1):
            run = one * run + est_last[c]
        pt_last[z] = run
        for q in range(1, Z):
            @pl.when(goes(1, q))
            def _():
                last_line_send(q).start()

    def enter_last():
        for q in range(1, Z):
            @pl.when(comes(1, q))
            def _():
                last_line_recv(q).wait_recv()
        dec_all = dec_ref[:, chunk(LAST)]
        one = decay_rows(dec_all, float(T))
        four = decay_rows(dec_all, float(4 * T))
        run = jnp.zeros((modes, ck), jnp.float32)
        far = run
        for zz in range(Z - 1, -1, -1):
            far = jnp.where(z == zz, run, far)
            run = four * run + pt_last[zz]
        mine_in = far
        for c in range(3, -1, -1):
            mine_in = jnp.where(xc == c, far, mine_in)
            far = one * far + est_last[c]
        entry[1, LAST] = mine_in

    def late(w, k):
        @pl.when(xc == owner(k))
        def _():
            for q in range(1, Z):
                @pl.when(comes(w, q))
                def _():
                    line_recv(w, k, q).wait_recv()
            dec_all = dec_ref[:, chunk(k)]
            one = decay_rows(dec_all, float(T))
            four = decay_rows(dec_all, float(4 * T))
            run = jnp.zeros((modes, ck), jnp.float32)
            far = run
            for zz in (range(Z) if w == 0 else range(Z - 1, -1, -1)):
                far = jnp.where(z == zz, run, far)
                run = four * run + pt[w, k // 4, zz]
            for c in (range(4) if w == 0 else range(3, -1, -1)):
                after = one * far + est[w, k // 4, c]
                est[w, k // 4, c] = far
                far = after
            entry[w, k] = est[w, k // 4, xc]
            for q in (1, 2, 3):
                enter_send(w, k, q).start()

    def second_pass(w, k, src, ring, slot, out):
        @pl.when((xc != owner(k)) & (True if w == 0 else k != LAST))
        def _():
            enter_recv(w, k).wait_recv()
        entering = entry[w, k]
        row = lax.broadcasted_iota(jnp.int32, (8, 128), 0)
        seg = (row if w == 0 else 7 - row).astype(jnp.float32) * float(-L)
        for g in range(LG):
            dec = dec_ref[:, lanes(k, g)]
            res = res_ref[:, lanes(k, g)]
            init = []
            for m in range(modes):
                carried = entering[m:m + 1, g * 128:(g + 1) * 128]
                init.append(ring[slot, g, m] + jnp.exp(dec[m:m + 1] * seg) * carried)
            segment_run(src.at[slot, g], dec, res, init, out.at[g], L, w == 1)

    def fwd_first(k):
        load_x(k).wait()

        @pl.when(k + 1 < NK)
        def _():
            load_x(k + 1).start()
        slot = lax.rem(k, xs.shape[0])
        v = xin[lax.rem(k, xin.shape[0])].astype(jnp.float32)
        for g in range(LG):
            xs[slot, g] = v[:, g * 128:(g + 1) * 128]
        first_pass(0, k, xs, enf, slot)

    def fwd_second(k):
        second_pass(0, k, xs, enf, lax.rem(k, xs.shape[0]), conv.at[k])

    def back_first(k):
        psend(k).wait_recv()
        load_q(k).wait()

        @pl.when(k + 1 < NK)
        def _():
            load_q(k + 1).start()
        @pl.when(k >= 2)
        def _():
            store_q(k - 2).wait()
        slot = lax.rem(k, gs.shape[0])
        scale = pbuf[k, T:T + PAD, :].astype(jnp.float32)[0:1]

        def gates(b, c):
            r = pl.ds(pl.multiple_of(b * 32, 32), 32)
            mixed = own[lax.rem(k, own.shape[0]), r, :] + decode(pbuf[k, r, :], scale)
            gate = qin[lax.rem(k, qin.shape[0]), r, :].astype(jnp.float32)
            for g in range(LG):
                sl = slice(g * 128, (g + 1) * 128)
                oq[lax.rem(k, 2), r, sl] = (mixed[:, sl] * conv[k, g, r, :]).astype(jnp.bfloat16)
                gs[slot, g, r, :] = mixed[:, sl] * gate[:, sl]
            return c
        lax.fori_loop(0, T // 32, gates, 0)
        store_q(k).start()
        first_pass(1, k, gs, enb, slot)

    def back_second(k):
        second_pass(1, k, gs, enb, lax.rem(k, gs.shape[0]), ys)

        @pl.when(k >= 2)
        def _():
            store_i(k - 2).wait()
        for g in range(LG):
            oi[lax.rem(k, 2), :, g * 128:(g + 1) * 128] = ys[g].astype(jnp.bfloat16)
        store_i(k).start()

    load_x(0).start()
    load_q(0).start()
    for zz in range(Z):
        @pl.when(zz > z)
        def _():
            pt[0, :, zz] = jnp.zeros((NK // 4, modes, ck), jnp.float32)

        @pl.when(zz < z)
        def _():
            pt[1, :, zz] = jnp.zeros((NK // 4, modes, ck), jnp.float32)
            pt_last[zz] = jnp.zeros((modes, ck), jnp.float32)

    def span(k, start, behind, f, end=NK):
        def upto(t):
            return jnp.maximum(jnp.minimum(jnp.minimum(2 * (t - start + 1), t - behind + 1), end), 0)

        def body(t, c):
            f(t)
            return c
        lax.fori_loop(upto(k - 1), upto(k), body, 0)

    def guard(k, f):
        @pl.when((k >= 0) & (k < NK))
        def _():
            f(k)

    def loop(k, c):
        guard(k, step_a)

        @pl.when(k == lag)
        def _():
            g_wait()
        span(k, lag, 2, matmul)
        guard(k, fwd_first)
        guard(k - 1, step_b)
        guard(k - 1, lambda t: middle(0, t))
        guard(k - 2, lambda t: late(0, t))
        guard(k - 3, fwd_second)
        span(k, lag + 1, 3, back_first)
        span(k, lag + 2, 4, lambda t: middle(1, t), LAST)

        @pl.when(k == NK + 3)
        def _():
            middle_last()
        span(k, lag + 3, 5, lambda t: late(1, t), LAST)
        span(k, lag + 4, 6, back_second, LAST)
        return c
    lax.fori_loop(0, NK + 5, loop, 0)
    enter_last()
    back_second(LAST)

    def drain(k, c):
        @pl.when(k >= NK - NS)
        def _():
            psend(k).wait_send()

        @pl.when(k >= NK - 2)
        def _():
            store_q(k).wait()
            store_i(k).wait()
        zsend(k).wait_send()
        xfwd(k, 0).wait_send()
        xfwd(k, 1).wait_send()
        sib(k, 0).wait_send()
        sib(k, 1).wait_send()
        for w in range(2):
            chained = True if w == 0 else k != LAST

            @pl.when((xc != owner(k)) & chained)
            def _():
                end_send(w, k).wait_send()

            @pl.when((xc == owner(k)) & chained)
            def _():
                for q in (1, 2, 3):
                    enter_send(w, k, q).wait_send()
                for q in range(1, Z):
                    @pl.when(goes(w, q))
                    def _():
                        line_send(w, k, q).wait_send()
        return c
    lax.fori_loop(0, NK, drain, 0)
    for q in (1, 2, 3):
        last_send(q).wait_send()
    for q in range(1, Z):
        @pl.when(goes(1, q))
        def _():
            last_line_send(q).wait_send()
    for p in range(GP):
        def b():
            g_part(p).wait_send()

        def c():
            for d in range(1, C):
                g_own(p, d).wait_send()
                g_fwd(p, d).wait_send()
        guarded(other, b)
        guarded(mine, c)


def on_device(gated_input, query, out_grad, out_weight, decay_rate, residue, n, C,
              ck=256, GP=4, lag=4, win=2, pre=4, NS=4):
    T, fw = out_grad.shape
    cw, fb = out_weight.shape
    modes = decay_rate.shape[0]
    NK = cw // ck
    Z = n // 4
    lag = min(lag, NK - 1)
    split = n // C >= 8
    gcols, NG = (fw // 2, C) if split else (fw, C // 2)
    NS = min(NS, NK)
    LG = ck // 128
    cfg = (C, NK, ck, T, gcols, NG, fb, GP, lag, win, pre, NS, Z)
    S = pltpu.SemaphoreType.DMA
    bf, f32 = jnp.bfloat16, jnp.float32
    V = pltpu.VMEM
    any_spec = pl.BlockSpec(memory_space=pl.ANY)
    vmem_spec = pl.BlockSpec(memory_space=pltpu.VMEM)
    return pl.pallas_call(
        functools.partial(kernel, cfg),
        out_shape=(jax.ShapeDtypeStruct((T, cw), bf), jax.ShapeDtypeStruct((T, cw), bf)),
        in_specs=[any_spec] * 4 + [vmem_spec] * 2,
        out_specs=(any_spec, any_spec),
        scratch_shapes=[
            V((NK, 4, 2, ck, fb), bf),
            V((2, NG, T, gcols), bf),
            V((NK, T + PAD, ck), bf),
            V((NS, T + PAD, ck), bf),
            V((2 * T, ck), f32),
            V((6, T, ck), f32),
            V((NK, LG, T, 128), f32),
            V((2, T, ck), bf), V((2, T, ck), bf),
            V((4, LG, T, 128), f32), V((8, LG, T, 128), f32), V((LG, T, 128), f32),
            V((4, LG, modes, 8, 128), f32), V((8, LG, modes, 8, 128), f32),
            V((2, NK, modes, ck), f32), V((2, NK // 4, 4, modes, ck), f32),
            V((2, NK // 4, Z, modes, ck), f32), V((2, NK, modes, ck), f32),
            V((4, modes, ck), f32), V((Z, modes, ck), f32),
            V((2, T, ck), bf), V((2, T, ck), bf),
            S((NK + 1,)),
            S((2, C, GP)), S((2, C, GP)),
            S((NK,)), S((NK,)),
            S((NK, 2)), S((NK, 2)),
            S((NK, 2)), S((NK, 2)),
            S((NK,)), S((NK,)),
            S((2, NK)), S((2, NK, 4)),
            S((2, NK, Z)), S((2, NK, Z)),
            S((2, NK, 4)), S((2, NK)),
            S((4,)), S((4,)), S((Z,)), S((Z,)),
            S((2,)), S((2,)), S((2,)), S((2,)),
        ],
        compiler_params=pltpu.CompilerParams(collective_id=0, has_side_effects=True, vmem_limit_bytes=60 * 1024 * 1024),
    )(out_grad, out_weight, gated_input, query, decay_rate, residue)


def solution(mesh):
    return jax.shard_map(
        functools.partial(on_device, n=mesh.shape["ctx"], C=mesh.shape["chan"]),
        mesh=mesh,
        in_specs=(
            P("ctx", "chan"),
            P("ctx", "chan"),
            P("ctx", "chan"),
            P("chan", "ctx"),
            P(None, "chan"),
            P(None, "chan"),
        ),
        out_specs=(P("ctx", "chan"), P("ctx", "chan")),
        check_vma=False,
    )
```
